32 devices in a mesh: space: 4 (over z), energy: 8 (over y, x, core).
Axes of the slice: x: 2, y: 2, z: 4, core: 2. Of those that a mesh axis runs over, the one named last changes fastest.
Arguments:
- onsite: float32 [16, 4, 128], P('energy', 'space'), parts along dimension 0, may hold values from -0.8 to 0.8, as said below
- hopping: float32 [16, 4, 128, 128], P('energy', 'space'), parts along dimension 0, may hold values from -0.25 to 0.25, as said below
- coupling: float32 [16, 4, 128, 128], P('energy', 'space'), parts along dimension 0, may hold values from -0.25 to 0.75
Outputs:
- retarded: float32 [16, 4, 128, 128], P('energy', 'space'), parts along dimension 0
The draws below stay inside these ranges and needn't reach their ends.
There are 8 independent parts, one for each index of `energy`. The reference program is written for one: setup_inputs(seed, part) draws one part's arguments, and reference() takes and returns one part's arrays. A program takes and returns all parts, laid end to end along the dimension named above; each array names one. Nothing has to cross between parts.
Inputs may be any that keep to these rules, and one draw needn't show every extreme that they name: Row 1 of onsite (the imaginary parts) lies between 0.002 and 0.01. Every slab's block is Hermitian: hopping[0, k] is symmetric and hopping[1, k] antisymmetric in the last two dimensions.
All inputs are finite; a program needn't handle non-finite values.
Results may differ from the reference program's by a relative error of at most 0.0014.
Values sent between devices are 32-bit elements; how exact they have to be, the bound alone decides.
No kernel may reach another device: no remote copies, remote signals or barrier semaphores. Data moves between devices by JAX's collectives and lax.ppermute only.
A program may use at most 64 MiB of HBM per device.

```python
import math
import jax
import jax.numpy as jnp
from jax import lax

B = 128
NS = 4


def draw_onsite(key, part):
    key_shift, key_real, key_imag = jax.random.split(key, 3)
    energy_shift = jax.random.uniform(key_shift, (), jnp.float32, -0.4, 0.4)
    real_part = energy_shift + jax.random.uniform(key_real, (NS, B), jnp.float32, -0.2, 0.2)
    imaginary = 0.002 * jnp.exp(jax.random.uniform(key_imag, (NS, B), jnp.float32, 0.0, math.log(5.0)))
    return jnp.stack([real_part, imaginary])


def draw_hopping(key, part):
    key_real, key_imag = jax.random.split(key)
    spread = 0.15 / math.sqrt(2.0 * B)
    real_part = spread * jax.random.normal(key_real, (NS, B, B), jnp.float32)
    imaginary = spread * jax.random.normal(key_imag, (NS, B, B), jnp.float32)
    symmetric = (real_part + jnp.swapaxes(real_part, 1, 2)) / math.sqrt(2.0)
    antisymmetric = (imaginary - jnp.swapaxes(imaginary, 1, 2)) / math.sqrt(2.0)
    return jnp.clip(jnp.stack([symmetric, antisymmetric]), -0.25, 0.25)


def draw_coupling(key, part):
    key_real, key_imag = jax.random.split(jax.random.fold_in(key, 7))
    spread = 0.15 / math.sqrt(2.0 * B)
    identity_block = 0.5 * jnp.eye(B, dtype=jnp.float32)[None, :, :]
    real_noise = spread * jax.random.normal(key_real, (NS, B, B), jnp.float32)
    imaginary = spread * jax.random.normal(key_imag, (NS, B, B), jnp.float32)
    real_part = identity_block + real_noise
    return jnp.clip(jnp.stack([real_part, imaginary]), -0.25, 0.75)


def setup_inputs(seed: int = 0, part: int = 0) -> dict:
    splits = jax.random.split(jax.random.key(seed), 4)
    part_splits = jax.random.split(jax.random.fold_in(splits[3], part), 4)
    return {
        "onsite": draw_onsite(jax.random.fold_in(jax.random.fold_in(splits[3], part), 71), part),
        "hopping": draw_hopping(jax.random.fold_in(jax.random.fold_in(splits[3], part), 71), part),
        "coupling": draw_coupling(jax.random.fold_in(jax.random.fold_in(splits[3], part), 71), part),
    }


def matmul_exact(former, latter):
    return jnp.matmul(former, latter, precision=lax.Precision.HIGHEST)

def complex_product(former, latter):
    real_part = matmul_exact(former[0], latter[0]) - matmul_exact(former[1], latter[1])
    imaginary = matmul_exact(former[0], latter[1]) + matmul_exact(former[1], latter[0])
    return jnp.stack([real_part, imaginary])

def adjoint(matrix):
    return jnp.stack([matrix[0].T, -matrix[1].T])

def invert(matrix):
    orbitals = matrix.shape[-1]
    embedded = jnp.concatenate([jnp.concatenate([matrix[0], -matrix[1]], 1), jnp.concatenate([matrix[1], matrix[0]], 1)], 0)
    solved = jnp.linalg.solve(embedded, jnp.eye(2 * orbitals, dtype=matrix.dtype))
    return jnp.stack([solved[:orbitals, :orbitals], solved[orbitals:, :orbitals]])

def reference(onsite, hopping, coupling):
    orbitals = onsite.shape[-1]
    diagonal = jax.vmap(jnp.diag)
    blocks = jnp.stack([diagonal(onsite[0]) - hopping[0], diagonal(onsite[1]) - hopping[1]], 1)
    links = jnp.moveaxis(coupling, 0, 1)
    contact = jnp.stack([jnp.zeros((orbitals, orbitals), onsite.dtype), -jnp.eye(orbitals, dtype=onsite.dtype)])

    def advance(previous, item):
        slab_block, slab_link = item
        sigma = complex_product(adjoint(slab_link), complex_product(previous, slab_link))
        fresh = invert(slab_block - sigma)
        return (fresh, fresh)
    _, left_greens = lax.scan(advance, contact, (blocks, links))

    def recede(later_green, item):
        left_green, slab_link = item
        outward = complex_product(left_green, slab_link)
        inward = complex_product(adjoint(slab_link), left_green)
        full = left_green + complex_product(outward, complex_product(later_green, inward))
        return (full, full)
    closing = left_greens[-1]
    _, earlier = lax.scan(recede, closing, (left_greens[:-1], links[1:]), reverse=True)
    return jnp.moveaxis(jnp.concatenate([earlier, closing[None]], 0), 1, 0)
```

```python
import functools

import jax
import jax.numpy as jnp
from jax import lax
from jax.experimental import pallas as pl
from jax.experimental.pallas import tpu as pltpu
from jax.sharding import PartitionSpec as P

TILE = 8


def dot_full(former, latter):
    return jnp.dot(former, latter, precision=lax.Precision.HIGHEST, preferred_element_type=jnp.float32)


def halves(value):
    high = value.astype(jnp.bfloat16)
    return high, (value - high.astype(jnp.float32)).astype(jnp.bfloat16)


def dot_halves(former, latter):
    former_high, former_low = halves(former)
    latter_high, latter_low = halves(latter)
    dot = functools.partial(jnp.dot, preferred_element_type=jnp.float32)
    return dot(former_high, latter_high) + (dot(former_high, latter_low) + dot(former_low, latter_high))


def complex_product(former, latter, dot=dot_full):
    columns = latter[0].shape[1]
    wide = jnp.concatenate(former, axis=1)
    top = jnp.concatenate(latter, axis=1)
    bottom = jnp.concatenate([-latter[1], latter[0]], axis=1)
    both = dot(wide, jnp.concatenate([top, bottom], axis=0))
    return both[:, :columns], both[:, columns:]


def adjoint(value):
    return value[0].T, -value[1].T


def minus(former, latter):
    return former[0] - latter[0], former[1] - latter[1]


def plus(former, latter):
    return former[0] + latter[0], former[1] + latter[1]


def load(ref):
    return ref[0], ref[1]


def store(ref, value):
    ref[0] = value[0]
    ref[1] = value[1]


def times(ar, ai, br, bi):
    return ar * br - ai * bi, ar * bi + ai * br


def gauss_jordan(re, im):
    size = re.shape[0]
    lane = lax.broadcasted_iota(jnp.int32, (TILE, size), 1)
    sub = lax.broadcasted_iota(jnp.int32, (TILE, size), 0)
    lane_all = lax.broadcasted_iota(jnp.int32, (size, size), 1)

    def column(value, index):
        return jnp.broadcast_to(value[:, index : index + 1], (TILE, size))

    def row(value, index):
        return jnp.broadcast_to(value[index : index + 1, :], (TILE, size))

    past = None
    for start in range(0, size, TILE):
        stop = start + TILE
        pr, pi = re[start:stop, :], im[start:stop, :]
        if past is not None:
            first = start - TILE
            own = (lane >= first) & (lane < start)
            terms = [
                times(column(pr, first + k), column(pi, first + k), row(past[0], k), row(past[1], k))
                for k in range(TILE)
            ]
            while len(terms) > 1:
                terms = [plus(a, b) for a, b in zip(terms[::2], terms[1::2])]
            pr, pi = minus((jnp.where(own, 0.0, pr), jnp.where(own, 0.0, pi)), terms[0])
        spread = [
            (
                jnp.where(sub > TILE, 0.0, column(pr, start + j)),
                jnp.where(sub > TILE, 0.0, column(pi, start + j)),
            )
            for j in range(TILE)
        ]
        for j in range(TILE):
            br, bi = spread[j]
            xr, xi = row(br, j), row(bi, j)
            scale = 1.0 / (xr * xr + xi * xi)
            qr, qi = xr * scale, -(xi * scale)
            at_row = sub == j
            ur, ui = times(br, bi, qr, qi)
            wr, wi = jnp.where(at_row, qr, -ur), jnp.where(at_row, qi, -ui)
            for k in range(j + 1, TILE):
                yr, yi = spread[k]
                tr, ti = times(wr, wi, row(yr, j), row(yi, j))
                spread[k] = (jnp.where(at_row, 0.0, yr) + tr, jnp.where(at_row, 0.0, yi) + ti)
            at_lane = lane == start + j
            tr = jnp.where(at_lane, 1.0, row(pr, j))
            ti = jnp.where(at_lane, 0.0, row(pi, j))
            tr, ti = times(wr, wi, tr, ti)
            clear = at_row | at_lane
            pr = jnp.where(clear, 0.0, pr) + tr
            pi = jnp.where(clear, 0.0, pi) + ti
        ar, ai = re[...], im[...]

        def padded(value, start=start, stop=stop):
            blocks = [value]
            if start:
                blocks.insert(0, jnp.zeros((start, size), jnp.float32))
            if stop < size:
                blocks.append(jnp.zeros((size - stop, size), jnp.float32))
            return jnp.concatenate(blocks, axis=0)

        ur, ui = complex_product((ar, ai), (padded(pr), padded(pi)), dot_halves)
        own = (lane_all >= start) & (lane_all < stop)
        nr = jnp.where(own, 0.0, ar) - ur
        ni = jnp.where(own, 0.0, ai) - ui
        for low, high in ((0, start), (min(stop + TILE, size), size)):
            if high > low:
                re[low:high, :] = nr[low:high]
                im[low:high, :] = ni[low:high]
        re[start:stop, :] = pr
        im[start:stop, :] = pi
        past = (pr, pi)


def inverse(matrix, re, im, refine=False):
    re[...] = matrix[0]
    im[...] = matrix[1]
    gauss_jordan(re, im)
    result = re[...], im[...]
    if refine:
        size = re.shape[0]
        diagonal = lax.broadcasted_iota(jnp.int32, (size, size), 0) == lax.broadcasted_iota(jnp.int32, (size, size), 1)
        pr, pi = complex_product(matrix, result)
        rest = jnp.where(diagonal, 1.0, 0.0) - pr, -pi
        result = plus(result, complex_product(result, rest, dot_halves))
    return result


def begin_kernel(place, onsite, hopping, coupling, matrix, green, re, im):
    size = re.shape[0]
    diagonal = lax.broadcasted_iota(jnp.int32, (size, size), 0) == lax.broadcasted_iota(jnp.int32, (size, size), 1)
    for part in range(2):
        spread = jnp.broadcast_to(onsite[part], (size, size))
        matrix[part] = jnp.where(diagonal, spread, 0.0) - hopping[part, 0]

    @pl.when(place[0] == 0)
    def _():
        link = coupling[0, 0], coupling[1, 0]
        pr, pi = complex_product(adjoint(link), link)
        matrix[0] = matrix[0] - pi
        matrix[1] = matrix[1] + pr

    store(green, inverse(load(matrix), re, im, refine=True))


def links_kernel(place, coupling, behind, inner, inner_adj, outer, outer_adj):
    own = coupling[0, 0], coupling[1, 0]
    other = behind[0, 0], behind[1, 0]

    @pl.when(place[1] == 1)
    def _():
        store(inner, own)
        store(inner_adj, adjoint(own))
        store(outer, adjoint(other))
        store(outer_adj, other)

    @pl.when(place[1] == 0)
    def _():
        store(outer, own)
        store(outer_adj, adjoint(own))
        store(inner, adjoint(other))
        store(inner_adj, other)


def advance_kernel(matrix, incoming, link, link_adj, reduced, green, re, im):
    sigma = complex_product(load(link_adj), complex_product(load(incoming), load(link)))
    value = minus(load(matrix), sigma)
    store(reduced, value)
    store(green, inverse(value, re, im, refine=True))


def meet_kernel(place, reduced, green, incoming, link, link_adj, full, before, after, re, im):
    @pl.when(place[2] == 1)
    def _():
        sigma = complex_product(load(link_adj), complex_product(load(incoming), load(link)))
        store(full, inverse(minus(load(reduced), sigma), re, im, refine=True))

    @pl.when(place[2] == 0)
    def _():
        store(full, load(green))
        store(before, complex_product(load(green), load(link_adj)))
        store(after, complex_product(load(link), load(green)))


def recede_kernel(place, full, green, incoming, before, after, out):
    @pl.when(place[2] == 1)
    def _():
        for part in range(2):
            out[part, 0] = full[part]

    @pl.when(place[2] == 0)
    def _():
        change = complex_product(complex_product(load(before), load(incoming)), load(after))
        value = plus(load(green), change)
        for part in range(2):
            out[part, 0] = value[part]


def on_device(onsite, hopping, coupling):
    assert onsite.shape[1] == 1
    size = onsite.shape[-1]
    pair = jax.ShapeDtypeStruct((2, size, size), jnp.float32)
    scratch = [pltpu.VMEM((size, size), jnp.float32)] * 2
    smem = pl.BlockSpec(memory_space=pltpu.SMEM)
    vmem = pl.BlockSpec(memory_space=pltpu.VMEM)

    def call(kernel, placed, inputs, outputs, scratches=(), **options):
        return pl.pallas_call(
            kernel,
            out_shape=(pair,) * outputs if outputs else jax.ShapeDtypeStruct((2, 1, size, size), jnp.float32),
            in_specs=([smem] if placed else []) + [vmem] * inputs,
            scratch_shapes=scratches,
        )

    count = lax.axis_size("space")
    position = lax.axis_index("space")
    half = count // 2
    is_left = position < half
    is_middle = (position == half - 1) | (position == half) if half else position == 0
    place = jnp.stack([position, is_left.astype(jnp.int32), is_middle.astype(jnp.int32)]).astype(jnp.int32)

    from_right = lax.ppermute(coupling, "space", [(k + 1, k) for k in range(count - 1)])
    matrix, green = call(begin_kernel, True, 3, 2, scratch)(place, onsite, hopping, coupling)
    from_right, _ = lax.optimization_barrier((from_right, green))
    inner, inner_adj, outer, outer_adj = call(links_kernel, True, 2, 4)(place, coupling, from_right)

    inward = [(k, k + 1) for k in range(half - 1)] + [(k, k - 1) for k in range(half + 1, count)]
    reduced = matrix
    for _ in range(max(half, count - half) - 1):
        incoming = lax.ppermute(green, "space", inward)
        reduced, green = call(advance_kernel, False, 4, 2, scratch)(matrix, incoming, inner, inner_adj)

    meeting = [(half - 1, half), (half, half - 1)] if half else []
    incoming = lax.ppermute(green, "space", meeting)
    full, before, after = call(meet_kernel, True, 5, 3, scratch)(place, reduced, green, incoming, outer, outer_adj)

    outward = [(k, k - 1) for k in range(1, half)] + [(k, k + 1) for k in range(half, count - 1)]
    result = full[:, None]
    for _ in range(max(half, count - half) - 1):
        incoming = lax.ppermute(result[:, 0], "space", outward)
        result = call(recede_kernel, True, 5, 0)(place, full, green, incoming, before, after)
    return result


def solution(mesh):
    return jax.shard_map(
        on_device,
        mesh=mesh,
        in_specs=(
            P("energy", "space", None),
            P("energy", "space", None, None),
            P("energy", "space", None, None),
        ),
        out_specs=P("energy", "space", None, None),
        check_vma=False,
    )
```

```python
import functools

import jax
import jax.numpy as jnp
from jax import lax
from jax.experimental import pallas as pl
from jax.experimental.pallas import tpu as pltpu
from jax.sharding import PartitionSpec as P

TILE = 8


def dot_full(former, latter):
    return jnp.dot(former, latter, precision=lax.Precision.HIGHEST, preferred_element_type=jnp.float32)


def halves(value):
    high = value.astype(jnp.bfloat16)
    return high, (value - high.astype(jnp.float32)).astype(jnp.bfloat16)


def dot_halves(former, latter):
    former_high, former_low = halves(former)
    latter_high, latter_low = halves(latter)
    dot = functools.partial(jnp.dot, preferred_element_type=jnp.float32)
    return dot(former_high, latter_high) + (dot(former_high, latter_low) + dot(former_low, latter_high))


def complex_product(former, latter, dot=dot_full):
    columns = latter[0].shape[1]
    wide = jnp.concatenate(former, axis=1)
    top = jnp.concatenate(latter, axis=1)
    bottom = jnp.concatenate([-latter[1], latter[0]], axis=1)
    both = dot(wide, jnp.concatenate([top, bottom], axis=0))
    return both[:, :columns], both[:, columns:]


def adjoint(value):
    return value[0].T, -value[1].T


def minus(former, latter):
    return former[0] - latter[0], former[1] - latter[1]


def plus(former, latter):
    return former[0] + latter[0], former[1] + latter[1]


def load(ref):
    return ref[0], ref[1]


def store(ref, value):
    ref[0] = value[0]
    ref[1] = value[1]


def times(ar, ai, br, bi):
    return ar * br - ai * bi, ar * bi + ai * br


def gauss_jordan(re, im):
    size = re.shape[0]
    lane = lax.broadcasted_iota(jnp.int32, (TILE, size), 1)
    sub = lax.broadcasted_iota(jnp.int32, (TILE, size), 0)
    lane_all = lax.broadcasted_iota(jnp.int32, (size, size), 1)

    def column(value, index):
        return jnp.broadcast_to(value[:, index : index + 1], (TILE, size))

    def row(value, index):
        return jnp.broadcast_to(value[index : index + 1, :], (TILE, size))

    past = None
    for start in range(0, size, TILE):
        stop = start + TILE
        pr, pi = re[start:stop, :], im[start:stop, :]
        if past is not None:
            first = start - TILE
            own = (lane >= first) & (lane < start)
            terms = [
                times(column(pr, first + k), column(pi, first + k), row(past[0], k), row(past[1], k))
                for k in range(TILE)
            ]
            while len(terms) > 1:
                terms = [plus(a, b) for a, b in zip(terms[::2], terms[1::2])]
            pr, pi = minus((jnp.where(own, 0.0, pr), jnp.where(own, 0.0, pi)), terms[0])
        spread = [
            (
                jnp.where(sub > TILE, 0.0, column(pr, start + j)),
                jnp.where(sub > TILE, 0.0, column(pi, start + j)),
            )
            for j in range(TILE)
        ]
        for j in range(TILE):
            br, bi = spread[j]
            xr, xi = row(br, j), row(bi, j)
            scale = 1.0 / (xr * xr + xi * xi)
            qr, qi = xr * scale, -(xi * scale)
            at_row = sub == j
            ur, ui = times(br, bi, qr, qi)
            wr, wi = jnp.where(at_row, qr, -ur), jnp.where(at_row, qi, -ui)
            for k in range(j + 1, TILE):
                yr, yi = spread[k]
                tr, ti = times(wr, wi, row(yr, j), row(yi, j))
                spread[k] = (jnp.where(at_row, 0.0, yr) + tr, jnp.where(at_row, 0.0, yi) + ti)
            at_lane = lane == start + j
            tr = jnp.where(at_lane, 1.0, row(pr, j))
            ti = jnp.where(at_lane, 0.0, row(pi, j))
            tr, ti = times(wr, wi, tr, ti)
            clear = at_row | at_lane
            pr = jnp.where(clear, 0.0, pr) + tr
            pi = jnp.where(clear, 0.0, pi) + ti
        ar, ai = re[...], im[...]

        def padded(value, start=start, stop=stop):
            blocks = [value]
            if start:
                blocks.insert(0, jnp.zeros((start, size), jnp.float32))
            if stop < size:
                blocks.append(jnp.zeros((size - stop, size), jnp.float32))
            return jnp.concatenate(blocks, axis=0)

        ur, ui = complex_product((ar, ai), (padded(pr), padded(pi)), dot_halves)
        own = (lane_all >= start) & (lane_all < stop)
        nr = jnp.where(own, 0.0, ar) - ur
        ni = jnp.where(own, 0.0, ai) - ui
        for low, high in ((0, start), (min(stop + TILE, size), size)):
            if high > low:
                re[low:high, :] = nr[low:high]
                im[low:high, :] = ni[low:high]
        re[start:stop, :] = pr
        im[start:stop, :] = pi
        past = (pr, pi)


def inverse(matrix, re, im, refine=False):
    re[...] = matrix[0]
    im[...] = matrix[1]
    gauss_jordan(re, im)
    result = re[...], im[...]
    if refine:
        size = re.shape[0]
        diagonal = lax.broadcasted_iota(jnp.int32, (size, size), 0) == lax.broadcasted_iota(jnp.int32, (size, size), 1)
        pr, pi = complex_product(matrix, result)
        rest = jnp.where(diagonal, 1.0, 0.0) - pr, -pi
        result = plus(result, complex_product(result, rest, dot_halves))
    return result


def begin_kernel(place, onsite, hopping, coupling, matrix, green, re, im):
    size = re.shape[0]
    diagonal = lax.broadcasted_iota(jnp.int32, (size, size), 0) == lax.broadcasted_iota(jnp.int32, (size, size), 1)
    for part in range(2):
        spread = jnp.broadcast_to(onsite[part], (size, size))
        matrix[part] = jnp.where(diagonal, spread, 0.0) - hopping[part, 0]

    @pl.when(place[0] == 0)
    def _():
        link = coupling[0, 0], coupling[1, 0]
        pr, pi = complex_product(adjoint(link), link)
        matrix[0] = matrix[0] - pi
        matrix[1] = matrix[1] + pr

    store(green, inverse(load(matrix), re, im, refine=True))


def links_kernel(place, coupling, behind, inner, inner_adj, outer, outer_adj):
    own = coupling[0, 0], coupling[1, 0]
    other = behind[0, 0], behind[1, 0]

    @pl.when(place[1] == 1)
    def _():
        store(inner, own)
        store(inner_adj, adjoint(own))
        store(outer, adjoint(other))
        store(outer_adj, other)

    @pl.when(place[1] == 0)
    def _():
        store(outer, own)
        store(outer_adj, adjoint(own))
        store(inner, adjoint(other))
        store(inner_adj, other)


def advance_kernel(matrix, incoming, link, link_adj, reduced, green, re, im):
    sigma = complex_product(load(link_adj), complex_product(load(incoming), load(link)))
    value = minus(load(matrix), sigma)
    store(reduced, value)
    store(green, inverse(value, re, im, refine=True))


def meet_kernel(place, reduced, green, incoming, link, link_adj, full, before, after, re, im):
    @pl.when(place[2] == 1)
    def _():
        sigma = complex_product(load(link_adj), complex_product(load(incoming), load(link)))
        store(full, inverse(minus(load(reduced), sigma), re, im, refine=True))

    @pl.when(place[2] == 0)
    def _():
        store(full, load(green))
        store(before, complex_product(load(green), load(link_adj)))
        store(after, complex_product(load(link), load(green)))


def recede_kernel(place, full, green, incoming, before, after, out):
    @pl.when(place[2] == 1)
    def _():
        for part in range(2):
            out[part, 0] = full[part]

    @pl.when(place[2] == 0)
    def _():
        change = complex_product(complex_product(load(before), load(incoming)), load(after))
        value = plus(load(green), change)
        for part in range(2):
            out[part, 0] = value[part]


def chain_of_slabs(onsite, hopping, coupling):
    size = onsite.shape[-1]
    pair = jax.ShapeDtypeStruct((2, size, size), jnp.float32)
    scratch = [pltpu.VMEM((size, size), jnp.float32)] * 2
    smem = pl.BlockSpec(memory_space=pltpu.SMEM)
    vmem = pl.BlockSpec(memory_space=pltpu.VMEM)

    def call(kernel, placed, inputs, outputs, scratches=(), **options):
        return pl.pallas_call(
            kernel,
            out_shape=(pair,) * outputs if outputs else jax.ShapeDtypeStruct((2, 1, size, size), jnp.float32),
            in_specs=([smem] if placed else []) + [vmem] * inputs,
            scratch_shapes=scratches,
        )

    count = lax.axis_size("space")
    position = lax.axis_index("space")
    half = count // 2
    is_left = position < half
    is_middle = (position == half - 1) | (position == half) if half else position == 0
    place = jnp.stack([position, is_left.astype(jnp.int32), is_middle.astype(jnp.int32)]).astype(jnp.int32)

    from_right = lax.ppermute(coupling, "space", [(k + 1, k) for k in range(count - 1)])
    matrix, green = call(begin_kernel, True, 3, 2, scratch)(place, onsite, hopping, coupling)
    from_right, _ = lax.optimization_barrier((from_right, green))
    inner, inner_adj, outer, outer_adj = call(links_kernel, True, 2, 4)(place, coupling, from_right)

    inward = [(k, k + 1) for k in range(half - 1)] + [(k, k - 1) for k in range(half + 1, count)]
    reduced = matrix
    for _ in range(max(half, count - half) - 1):
        incoming = lax.ppermute(green, "space", inward)
        reduced, green = call(advance_kernel, False, 4, 2, scratch)(matrix, incoming, inner, inner_adj)

    meeting = [(half - 1, half), (half, half - 1)] if half else []
    incoming = lax.ppermute(green, "space", meeting)
    full, before, after = call(meet_kernel, True, 5, 3, scratch)(place, reduced, green, incoming, outer, outer_adj)

    outward = [(k, k - 1) for k in range(1, half)] + [(k, k + 1) for k in range(half, count - 1)]
    result = full[:, None]
    for _ in range(max(half, count - half) - 1):
        incoming = lax.ppermute(result[:, 0], "space", outward)
        result = call(recede_kernel, True, 5, 0)(place, full, green, incoming, before, after)
    return result


def choose(condition, former, latter):
    return jnp.where(condition, former[0], latter[0]), jnp.where(condition, former[1], latter[1])


def open_kernel(onsite, hopping, coupling, message, re, im):
    position = lax.axis_index("space")
    is_outer = (position == 0) | (position == 3)
    size = re.shape[0]
    diagonal = lax.broadcasted_iota(jnp.int32, (size, size), 0) == lax.broadcasted_iota(jnp.int32, (size, size), 1)
    for part in range(2):
        spread = jnp.broadcast_to(onsite[part], (size, size))
        message[part] = jnp.where(diagonal, spread, 0.0) - hopping[part, 0]
        message[2 + part] = coupling[part, 0]

    @pl.when(position == 0)
    def _():
        link = message[2], message[3]
        pr, pi = complex_product(adjoint(link), link)
        message[0] = message[0] - pi
        message[1] = message[1] + pr

    @pl.when(is_outer)
    def _():
        store(message, inverse(load(message), re, im, refine=True))


def half_kernel(mine, theirs, reduced, before, after, message, re, im):
    position = lax.axis_index("space")
    is_left = position < 2
    is_outer = (position == 0) | (position == 3)
    end = choose(is_outer, (mine[0], mine[1]), (theirs[0], theirs[1]))
    inner = choose(is_outer, (theirs[0], theirs[1]), (mine[0], mine[1]))
    use_mine = is_left ^ is_outer
    link = choose(use_mine, (mine[2], mine[3]), (theirs[2], theirs[3]))
    link_adj = adjoint(link)
    inward = choose(is_left, link, link_adj)
    outward = choose(is_left, link_adj, link)
    ahead = complex_product(end, inward)
    store(before, ahead)
    store(after, complex_product(outward, end))
    value = minus(inner, complex_product(outward, ahead))
    store(reduced, value)
    green = inverse(value, re, im, refine=True)
    store(message, green)

    @pl.when(jnp.logical_not(is_left))
    def _():
        middle = choose(is_outer, (theirs[2], theirs[3]), (mine[2], mine[3]))
        store(message, complex_product(complex_product(middle, load(message)), adjoint(middle)))


def close_kernel(mine, theirs, reduced, before, after, incoming, out, full, re, im):
    position = lax.axis_index("space")
    is_left = position < 2
    is_outer = (position == 0) | (position == 3)
    store(full, load(incoming))

    @pl.when(jnp.logical_not(is_left))
    def _():
        middle = choose(is_outer, (theirs[2], theirs[3]), (mine[2], mine[3]))
        store(full, complex_product(adjoint(middle), complex_product(load(incoming), middle)))

    green = inverse(minus(load(reduced), load(full)), re, im, refine=True)

    @pl.when(jnp.logical_not(is_outer))
    def _():
        out[0, 0] = green[0]
        out[1, 0] = green[1]

    @pl.when(is_outer)
    def _():
        store(full, green)
        change = complex_product(complex_product(load(before), load(full)), load(after))
        out[0, 0] = mine[0] + change[0]
        out[1, 0] = mine[1] + change[1]


def four_slabs(onsite, hopping, coupling):
    size = onsite.shape[-1]
    scratch = [pltpu.VMEM((size, size), jnp.float32)] * 2
    pair = pltpu.VMEM((2, size, size), jnp.float32)
    vmem = pl.BlockSpec(memory_space=pltpu.VMEM)

    def on_chip(value):
        return pltpu.with_memory_space_constraint(value, pltpu.VMEM)

    mine = pl.pallas_call(
        open_kernel, out_shape=pltpu.VMEM((4, size, size), jnp.float32), in_specs=[vmem] * 3, scratch_shapes=scratch
    )(onsite, hopping, coupling)
    theirs = on_chip(lax.ppermute(mine, "space", [(0, 1), (1, 0), (2, 3), (3, 2)]))
    reduced, before, after, message = pl.pallas_call(
        half_kernel, out_shape=(pair,) * 4, in_specs=[vmem] * 2, scratch_shapes=scratch
    )(mine, theirs)
    incoming = on_chip(lax.ppermute(message, "space", [(0, 3), (3, 0), (1, 2), (2, 1)]))
    return pl.pallas_call(
        close_kernel,
        out_shape=jax.ShapeDtypeStruct(hopping.shape, jnp.float32),
        in_specs=[vmem] * 6,
        scratch_shapes=[pltpu.VMEM((2, size, size), jnp.float32)] + scratch,
    )(mine, theirs, reduced, before, after, incoming)


def on_device(onsite, hopping, coupling):
    assert onsite.shape[1] == 1
    if lax.axis_size("space") == 4:
        return four_slabs(onsite, hopping, coupling)
    return chain_of_slabs(onsite, hopping, coupling)


def solution(mesh):
    return jax.shard_map(
        on_device,
        mesh=mesh,
        in_specs=(
            P("energy", "space", None),
            P("energy", "space", None, None),
            P("energy", "space", None, None),
        ),
        out_specs=P("energy", "space", None, None),
        check_vma=False,
    )
```

```python
import functools

import jax
import jax.numpy as jnp
from jax import lax
from jax.experimental import pallas as pl
from jax.experimental.pallas import tpu as pltpu
from jax.sharding import PartitionSpec as P

TILE = 8


def dot_full(former, latter):
    return jnp.dot(former, latter, precision=lax.Precision.HIGHEST, preferred_element_type=jnp.float32)


def halves(value):
    high = value.astype(jnp.bfloat16)
    return high, (value - high.astype(jnp.float32)).astype(jnp.bfloat16)


def dot_halves(former, latter):
    former_high, former_low = halves(former)
    latter_high, latter_low = halves(latter)
    dot = functools.partial(jnp.dot, preferred_element_type=jnp.float32)
    return dot(former_high, latter_high) + (dot(former_high, latter_low) + dot(former_low, latter_high))


def complex_product(former, latter, dot=dot_full):
    columns = latter[0].shape[1]
    wide = jnp.concatenate(former, axis=1)
    top = jnp.concatenate(latter, axis=1)
    bottom = jnp.concatenate([-latter[1], latter[0]], axis=1)
    both = dot(wide, jnp.concatenate([top, bottom], axis=0))
    return both[:, :columns], both[:, columns:]


def adjoint(value):
    return value[0].T, -value[1].T


def minus(former, latter):
    return former[0] - latter[0], former[1] - latter[1]


def plus(former, latter):
    return former[0] + latter[0], former[1] + latter[1]


def load(ref):
    return ref[0], ref[1]


def store(ref, value):
    ref[0] = value[0]
    ref[1] = value[1]


def times(ar, ai, br, bi):
    return ar * br - ai * bi, ar * bi + ai * br


def gauss_jordan(re, im):
    size = re.shape[0]
    lane = lax.broadcasted_iota(jnp.int32, (TILE, size), 1)
    sub = lax.broadcasted_iota(jnp.int32, (TILE, size), 0)
    lane_all = lax.broadcasted_iota(jnp.int32, (size, size), 1)

    def column(value, index):
        return jnp.broadcast_to(value[:, index : index + 1], (TILE, size))

    def row(value, index):
        return jnp.broadcast_to(value[index : index + 1, :], (TILE, size))

    past = None
    for start in range(0, size, TILE):
        stop = start + TILE
        pr, pi = re[start:stop, :], im[start:stop, :]
        if past is not None:
            first = start - TILE
            own = (lane >= first) & (lane < start)
            terms = [
                times(column(pr, first + k), column(pi, first + k), row(past[0], k), row(past[1], k))
                for k in range(TILE)
            ]
            while len(terms) > 1:
                terms = [plus(a, b) for a, b in zip(terms[::2], terms[1::2])]
            pr, pi = minus((jnp.where(own, 0.0, pr), jnp.where(own, 0.0, pi)), terms[0])
        spread = [
            (
                jnp.where(sub > TILE, 0.0, column(pr, start + j)),
                jnp.where(sub > TILE, 0.0, column(pi, start + j)),
            )
            for j in range(TILE)
        ]
        for j in range(TILE):
            br, bi = spread[j]
            xr, xi = row(br, j), row(bi, j)
            scale = 1.0 / (xr * xr + xi * xi)
            qr, qi = xr * scale, -(xi * scale)
            at_row = sub == j
            ur, ui = times(br, bi, qr, qi)
            wr, wi = jnp.where(at_row, qr, -ur), jnp.where(at_row, qi, -ui)
            for k in range(j + 1, TILE):
                yr, yi = spread[k]
                tr, ti = times(wr, wi, row(yr, j), row(yi, j))
                spread[k] = (jnp.where(at_row, 0.0, yr) + tr, jnp.where(at_row, 0.0, yi) + ti)
            at_lane = lane == start + j
            tr = jnp.where(at_lane, 1.0, row(pr, j))
            ti = jnp.where(at_lane, 0.0, row(pi, j))
            tr, ti = times(wr, wi, tr, ti)
            clear = at_row | at_lane
            pr = jnp.where(clear, 0.0, pr) + tr
            pi = jnp.where(clear, 0.0, pi) + ti
        ar, ai = re[...], im[...]

        def padded(value, start=start, stop=stop):
            blocks = [value]
            if start:
                blocks.insert(0, jnp.zeros((start, size), jnp.float32))
            if stop < size:
                blocks.append(jnp.zeros((size - stop, size), jnp.float32))
            return jnp.concatenate(blocks, axis=0)

        ur, ui = complex_product((ar, ai), (padded(pr), padded(pi)), dot_halves)
        own = (lane_all >= start) & (lane_all < stop)
        nr = jnp.where(own, 0.0, ar) - ur
        ni = jnp.where(own, 0.0, ai) - ui
        for low, high in ((0, start), (min(stop + TILE, size), size)):
            if high > low:
                re[low:high, :] = nr[low:high]
                im[low:high, :] = ni[low:high]
        re[start:stop, :] = pr
        im[start:stop, :] = pi
        past = (pr, pi)


def inverse(matrix, re, im, refine=False):
    re[...] = matrix[0]
    im[...] = matrix[1]
    gauss_jordan(re, im)
    result = re[...], im[...]
    if refine:
        size = re.shape[0]
        diagonal = lax.broadcasted_iota(jnp.int32, (size, size), 0) == lax.broadcasted_iota(jnp.int32, (size, size), 1)
        pr, pi = complex_product(matrix, result)
        rest = jnp.where(diagonal, 1.0, 0.0) - pr, -pi
        result = plus(result, complex_product(result, rest, dot_halves))
    return result


def begin_kernel(place, onsite, hopping, coupling, matrix, green, re, im):
    size = re.shape[0]
    diagonal = lax.broadcasted_iota(jnp.int32, (size, size), 0) == lax.broadcasted_iota(jnp.int32, (size, size), 1)
    for part in range(2):
        spread = jnp.broadcast_to(onsite[part], (size, size))
        matrix[part] = jnp.where(diagonal, spread, 0.0) - hopping[part, 0]

    @pl.when(place[0] == 0)
    def _():
        link = coupling[0, 0], coupling[1, 0]
        pr, pi = complex_product(adjoint(link), link)
        matrix[0] = matrix[0] - pi
        matrix[1] = matrix[1] + pr

    store(green, inverse(load(matrix), re, im, refine=True))


def links_kernel(place, coupling, behind, inner, inner_adj, outer, outer_adj):
    own = coupling[0, 0], coupling[1, 0]
    other = behind[0, 0], behind[1, 0]

    @pl.when(place[1] == 1)
    def _():
        store(inner, own)
        store(inner_adj, adjoint(own))
        store(outer, adjoint(other))
        store(outer_adj, other)

    @pl.when(place[1] == 0)
    def _():
        store(outer, own)
        store(outer_adj, adjoint(own))
        store(inner, adjoint(other))
        store(inner_adj, other)


def advance_kernel(matrix, incoming, link, link_adj, reduced, green, re, im):
    sigma = complex_product(load(link_adj), complex_product(load(incoming), load(link)))
    value = minus(load(matrix), sigma)
    store(reduced, value)
    store(green, inverse(value, re, im, refine=True))


def meet_kernel(place, reduced, green, incoming, link, link_adj, full, before, after, re, im):
    @pl.when(place[2] == 1)
    def _():
        sigma = complex_product(load(link_adj), complex_product(load(incoming), load(link)))
        store(full, inverse(minus(load(reduced), sigma), re, im, refine=True))

    @pl.when(place[2] == 0)
    def _():
        store(full, load(green))
        store(before, complex_product(load(green), load(link_adj)))
        store(after, complex_product(load(link), load(green)))


def recede_kernel(place, full, green, incoming, before, after, out):
    @pl.when(place[2] == 1)
    def _():
        for part in range(2):
            out[part, 0] = full[part]

    @pl.when(place[2] == 0)
    def _():
        change = complex_product(complex_product(load(before), load(incoming)), load(after))
        value = plus(load(green), change)
        for part in range(2):
            out[part, 0] = value[part]


def chain_of_slabs(onsite, hopping, coupling):
    size = onsite.shape[-1]
    pair = jax.ShapeDtypeStruct((2, size, size), jnp.float32)
    scratch = [pltpu.VMEM((size, size), jnp.float32)] * 2
    smem = pl.BlockSpec(memory_space=pltpu.SMEM)
    vmem = pl.BlockSpec(memory_space=pltpu.VMEM)

    def call(kernel, placed, inputs, outputs, scratches=(), **options):
        return pl.pallas_call(
            kernel,
            out_shape=(pair,) * outputs if outputs else jax.ShapeDtypeStruct((2, 1, size, size), jnp.float32),
            in_specs=([smem] if placed else []) + [vmem] * inputs,
            scratch_shapes=scratches,
        )

    count = lax.axis_size("space")
    position = lax.axis_index("space")
    half = count // 2
    is_left = position < half
    is_middle = (position == half - 1) | (position == half) if half else position == 0
    place = jnp.stack([position, is_left.astype(jnp.int32), is_middle.astype(jnp.int32)]).astype(jnp.int32)

    from_right = lax.ppermute(coupling, "space", [(k + 1, k) for k in range(count - 1)])
    matrix, green = call(begin_kernel, True, 3, 2, scratch)(place, onsite, hopping, coupling)
    from_right, _ = lax.optimization_barrier((from_right, green))
    inner, inner_adj, outer, outer_adj = call(links_kernel, True, 2, 4)(place, coupling, from_right)

    inward = [(k, k + 1) for k in range(half - 1)] + [(k, k - 1) for k in range(half + 1, count)]
    reduced = matrix
    for _ in range(max(half, count - half) - 1):
        incoming = lax.ppermute(green, "space", inward)
        reduced, green = call(advance_kernel, False, 4, 2, scratch)(matrix, incoming, inner, inner_adj)

    meeting = [(half - 1, half), (half, half - 1)] if half else []
    incoming = lax.ppermute(green, "space", meeting)
    full, before, after = call(meet_kernel, True, 5, 3, scratch)(place, reduced, green, incoming, outer, outer_adj)

    outward = [(k, k - 1) for k in range(1, half)] + [(k, k + 1) for k in range(half, count - 1)]
    result = full[:, None]
    for _ in range(max(half, count - half) - 1):
        incoming = lax.ppermute(result[:, 0], "space", outward)
        result = call(recede_kernel, True, 5, 0)(place, full, green, incoming, before, after)
    return result


def choose(condition, former, latter):
    return jnp.where(condition, former[0], latter[0]), jnp.where(condition, former[1], latter[1])


def whereabouts():
    position = lax.axis_index("space")
    return position < 2, (position == 0) | (position == 3)


def slab_kernel(onsite, hopping, coupling, mine):
    size = hopping.shape[-1]
    diagonal = lax.broadcasted_iota(jnp.int32, (size, size), 0) == lax.broadcasted_iota(jnp.int32, (size, size), 1)
    for part in range(2):
        spread = jnp.broadcast_to(onsite[part], (size, size))
        mine[part] = jnp.where(diagonal, spread, 0.0) - hopping[part, 0]
        mine[2 + part] = coupling[part, 0]


def end_kernel(mine, end, message, re, im):
    is_left, is_outer = whereabouts()

    @pl.when(is_outer)
    def _():
        link = mine[2], mine[3]
        store(end, (mine[0], mine[1]))

        @pl.when(is_left)
        def _():
            pr, pi = complex_product(adjoint(link), link)
            end[0] = end[0] - pi
            end[1] = end[1] + pr

        green = inverse(load(end), re, im, refine=True)
        store(end, green)
        store(message, green)

        @pl.when(jnp.logical_not(is_left))
        def _():
            store(message, complex_product(link, complex_product(load(end), adjoint(link))))


def send_half(is_left, middle, green, message):
    store(message, green)

    @pl.when(jnp.logical_not(is_left))
    def _():
        store(message, complex_product(middle, complex_product(load(message), adjoint(middle))))


def outer_kernel(mine, theirs, end, reduced, before, after, message, re, im):
    is_left, is_outer = whereabouts()

    @pl.when(is_outer)
    def _():
        link = choose(is_left, (theirs[2], theirs[3]), (mine[2], mine[3]))
        link_adj = adjoint(link)
        inward = choose(is_left, link, link_adj)
        outward = choose(is_left, link_adj, link)
        ahead = complex_product(load(end), inward)
        store(before, ahead)
        store(after, complex_product(outward, load(end)))
        value = minus((theirs[0], theirs[1]), complex_product(outward, ahead))
        store(reduced, value)
        send_half(is_left, (theirs[2], theirs[3]), inverse(value, re, im, refine=True), message)


def inner_kernel(mine, incoming, outer_reduced, outer_message, reduced, message, re, im):
    is_left, is_outer = whereabouts()

    @pl.when(is_outer)
    def _():
        store(reduced, load(outer_reduced))
        store(message, load(outer_message))

    @pl.when(jnp.logical_not(is_outer))
    def _():
        link = mine[2], mine[3]
        store(reduced, load(incoming))

        @pl.when(is_left)
        def _():
            store(reduced, complex_product(adjoint(link), complex_product(load(incoming), link)))

        value = minus((mine[0], mine[1]), load(reduced))
        store(reduced, value)
        send_half(is_left, link, inverse(value, re, im, refine=True), message)


def close_kernel(mine, theirs, end, before, after, reduced, incoming, out, full, re, im):
    is_left, is_outer = whereabouts()
    store(full, load(incoming))

    @pl.when(jnp.logical_not(is_left))
    def _():
        middle = choose(is_outer, (theirs[2], theirs[3]), (mine[2], mine[3]))
        store(full, complex_product(adjoint(middle), complex_product(load(incoming), middle)))

    green = inverse(minus(load(reduced), load(full)), re, im, refine=True)

    @pl.when(jnp.logical_not(is_outer))
    def _():
        out[0, 0] = green[0]
        out[1, 0] = green[1]

    @pl.when(is_outer)
    def _():
        store(full, green)
        change = complex_product(complex_product(load(before), load(full)), load(after))
        out[0, 0] = end[0] + change[0]
        out[1, 0] = end[1] + change[1]


def four_slabs(onsite, hopping, coupling):
    size = onsite.shape[-1]
    scratch = [pltpu.VMEM((size, size), jnp.float32)] * 2
    pair = pltpu.VMEM((2, size, size), jnp.float32)
    within_halves = [(0, 1), (1, 0), (2, 3), (3, 2)]
    across = [(0, 3), (3, 0), (1, 2), (2, 1)]

    def call(kernel, out_shape, scratch_shapes, *operands):
        vmem = pl.BlockSpec(memory_space=pltpu.VMEM)
        return pl.pallas_call(
            kernel, out_shape=out_shape, in_specs=[vmem] * len(operands), scratch_shapes=scratch_shapes
        )(*operands)

    def on_chip(*values):
        return [pltpu.with_memory_space_constraint(value, pltpu.VMEM) for value in values]

    mine = call(slab_kernel, pltpu.VMEM((4, size, size), jnp.float32), [], onsite, hopping, coupling)
    theirs = lax.ppermute(mine, "space", within_halves)
    mine, theirs = on_chip(mine, theirs)
    end, message = call(end_kernel, (pair,) * 2, scratch, mine)
    end, message = on_chip(end, message)
    incoming = on_chip(lax.ppermute(message, "space", within_halves))[0]
    outer = on_chip(*call(outer_kernel, (pair,) * 4, scratch, mine, theirs, end))
    inner = on_chip(*call(inner_kernel, (pair,) * 2, scratch, mine, incoming, outer[0], outer[3]))
    incoming = on_chip(lax.ppermute(inner[1], "space", across))[0]
    return call(
        close_kernel,
        jax.ShapeDtypeStruct(hopping.shape, jnp.float32),
        [pltpu.VMEM((2, size, size), jnp.float32)] + scratch,
        *(mine, theirs, end, outer[1], outer[2], inner[0], incoming),
    )


def on_device(onsite, hopping, coupling):
    assert onsite.shape[1] == 1
    if lax.axis_size("space") == 4:
        return four_slabs(onsite, hopping, coupling)
    return chain_of_slabs(onsite, hopping, coupling)


def solution(mesh):
    return jax.shard_map(
        on_device,
        mesh=mesh,
        in_specs=(
            P("energy", "space", None),
            P("energy", "space", None, None),
            P("energy", "space", None, None),
        ),
        out_specs=P("energy", "space", None, None),
        check_vma=False,
    )
```

```python
import functools

import jax
import jax.numpy as jnp
from jax import lax
from jax.experimental import pallas as pl
from jax.experimental.pallas import tpu as pltpu
from jax.sharding import PartitionSpec as P

TILE = 8


def dot_full(former, latter):
    return jnp.dot(former, latter, precision=lax.Precision.HIGHEST, preferred_element_type=jnp.float32)


def halves(value):
    high = value.astype(jnp.bfloat16)
    return high, (value - high.astype(jnp.float32)).astype(jnp.bfloat16)


def dot_halves(former, latter):
    former_high, former_low = halves(former)
    latter_high, latter_low = halves(latter)
    dot = functools.partial(jnp.dot, preferred_element_type=jnp.float32)
    return dot(former_high, latter_high) + (dot(former_high, latter_low) + dot(former_low, latter_high))


def complex_product(former, latter, dot=dot_full):
    columns = latter[0].shape[1]
    wide = jnp.concatenate(former, axis=1)
    top = jnp.concatenate(latter, axis=1)
    bottom = jnp.concatenate([-latter[1], latter[0]], axis=1)
    both = dot(wide, jnp.concatenate([top, bottom], axis=0))
    return both[:, :columns], both[:, columns:]


def adjoint(value):
    return value[0].T, -value[1].T


def minus(former, latter):
    return former[0] - latter[0], former[1] - latter[1]


def plus(former, latter):
    return former[0] + latter[0], former[1] + latter[1]


def load(ref):
    return ref[0], ref[1]


def store(ref, value):
    ref[0] = value[0]
    ref[1] = value[1]


def times(ar, ai, br, bi):
    return ar * br - ai * bi, ar * bi + ai * br


def gauss_jordan(re, im):
    size = re.shape[0]
    lane = lax.broadcasted_iota(jnp.int32, (TILE, size), 1)
    sub = lax.broadcasted_iota(jnp.int32, (TILE, size), 0)
    lane_all = lax.broadcasted_iota(jnp.int32, (size, size), 1)

    def column(value, index):
        return jnp.broadcast_to(value[:, index : index + 1], (TILE, size))

    def row(value, index):
        return jnp.broadcast_to(value[index : index + 1, :], (TILE, size))

    past = None
    for start in range(0, size, TILE):
        stop = start + TILE
        pr, pi = re[start:stop, :], im[start:stop, :]
        if past is not None:
            first = start - TILE
            own = (lane >= first) & (lane < start)
            terms = [
                times(column(pr, first + k), column(pi, first + k), row(past[0], k), row(past[1], k))
                for k in range(TILE)
            ]
            while len(terms) > 1:
                terms = [plus(a, b) for a, b in zip(terms[::2], terms[1::2])]
            pr, pi = minus((jnp.where(own, 0.0, pr), jnp.where(own, 0.0, pi)), terms[0])
        spread = [
            (
                jnp.where(sub > TILE, 0.0, column(pr, start + j)),
                jnp.where(sub > TILE, 0.0, column(pi, start + j)),
            )
            for j in range(TILE)
        ]
        pivot_re = pivot_im = pivot_scale = None
        for j in range(TILE):
            br, bi = spread[j]
            xr, xi = row(br, j), row(bi, j)
            scale = 1.0 / (xr * xr + xi * xi)
            at_row = sub == j
            wr = jnp.where(at_row, 0.0, (br * xr + bi * xi) * scale)
            wi = jnp.where(at_row, 0.0, (bi * xr - br * xi) * scale)
            for k in range(j + 1, TILE):
                yr, yi = spread[k]
                spread[k] = minus((yr, yi), times(wr, wi, row(yr, j), row(yi, j)))
            at_lane = lane == start + j
            tr, ti = times(wr, wi, row(pr, j), row(pi, j))
            pr = jnp.where(at_lane, jnp.where(at_row, 1.0, -wr), pr - tr)
            pi = jnp.where(at_lane, -wi, pi - ti)
            if j:
                xr = jnp.where(at_row, xr, pivot_re)
                xi = jnp.where(at_row, xi, pivot_im)
                scale = jnp.where(at_row, scale, pivot_scale)
            pivot_re, pivot_im, pivot_scale = xr, xi, scale
        pr, pi = times(pr, pi, pivot_re * pivot_scale, -(pivot_im * pivot_scale))
        ar, ai = re[...], im[...]

        def padded(value, start=start, stop=stop):
            blocks = [value]
            if start:
                blocks.insert(0, jnp.zeros((start, size), jnp.float32))
            if stop < size:
                blocks.append(jnp.zeros((size - stop, size), jnp.float32))
            return jnp.concatenate(blocks, axis=0)

        ur, ui = complex_product((ar, ai), (padded(pr), padded(pi)), dot_halves)
        own = (lane_all >= start) & (lane_all < stop)
        nr = jnp.where(own, 0.0, ar) - ur
        ni = jnp.where(own, 0.0, ai) - ui
        for low, high in ((0, start), (min(stop + TILE, size), size)):
            if high > low:
                re[low:high, :] = nr[low:high]
                im[low:high, :] = ni[low:high]
        re[start:stop, :] = pr
        im[start:stop, :] = pi
        past = (pr, pi)


def inverse(matrix, re, im, refine=False):
    re[...] = matrix[0]
    im[...] = matrix[1]
    gauss_jordan(re, im)
    result = re[...], im[...]
    if refine:
        size = re.shape[0]
        diagonal = lax.broadcasted_iota(jnp.int32, (size, size), 0) == lax.broadcasted_iota(jnp.int32, (size, size), 1)
        pr, pi = complex_product(matrix, result)
        rest = jnp.where(diagonal, 1.0, 0.0) - pr, -pi
        result = plus(result, complex_product(result, rest, dot_halves))
    return result


def begin_kernel(place, onsite, hopping, coupling, matrix, green, re, im):
    size = re.shape[0]
    diagonal = lax.broadcasted_iota(jnp.int32, (size, size), 0) == lax.broadcasted_iota(jnp.int32, (size, size), 1)
    for part in range(2):
        spread = jnp.broadcast_to(onsite[part], (size, size))
        matrix[part] = jnp.where(diagonal, spread, 0.0) - hopping[part, 0]

    @pl.when(place[0] == 0)
    def _():
        link = coupling[0, 0], coupling[1, 0]
        pr, pi = complex_product(adjoint(link), link)
        matrix[0] = matrix[0] - pi
        matrix[1] = matrix[1] + pr

    store(green, inverse(load(matrix), re, im, refine=True))


def links_kernel(place, coupling, behind, inner, inner_adj, outer, outer_adj):
    own = coupling[0, 0], coupling[1, 0]
    other = behind[0, 0], behind[1, 0]

    @pl.when(place[1] == 1)
    def _():
        store(inner, own)
        store(inner_adj, adjoint(own))
        store(outer, adjoint(other))
        store(outer_adj, other)

    @pl.when(place[1] == 0)
    def _():
        store(outer, own)
        store(outer_adj, adjoint(own))
        store(inner, adjoint(other))
        store(inner_adj, other)


def advance_kernel(matrix, incoming, link, link_adj, reduced, green, re, im):
    sigma = complex_product(load(link_adj), complex_product(load(incoming), load(link)))
    value = minus(load(matrix), sigma)
    store(reduced, value)
    store(green, inverse(value, re, im, refine=True))


def meet_kernel(place, reduced, green, incoming, link, link_adj, full, before, after, re, im):
    @pl.when(place[2] == 1)
    def _():
        sigma = complex_product(load(link_adj), complex_product(load(incoming), load(link)))
        store(full, inverse(minus(load(reduced), sigma), re, im, refine=True))

    @pl.when(place[2] == 0)
    def _():
        store(full, load(green))
        store(before, complex_product(load(green), load(link_adj)))
        store(after, complex_product(load(link), load(green)))


def recede_kernel(place, full, green, incoming, before, after, out):
    @pl.when(place[2] == 1)
    def _():
        for part in range(2):
            out[part, 0] = full[part]

    @pl.when(place[2] == 0)
    def _():
        change = complex_product(complex_product(load(before), load(incoming)), load(after))
        value = plus(load(green), change)
        for part in range(2):
            out[part, 0] = value[part]


def chain_of_slabs(onsite, hopping, coupling):
    size = onsite.shape[-1]
    pair = jax.ShapeDtypeStruct((2, size, size), jnp.float32)
    scratch = [pltpu.VMEM((size, size), jnp.float32)] * 2
    smem = pl.BlockSpec(memory_space=pltpu.SMEM)
    vmem = pl.BlockSpec(memory_space=pltpu.VMEM)

    def call(kernel, placed, inputs, outputs, scratches=(), **options):
        return pl.pallas_call(
            kernel,
            out_shape=(pair,) * outputs if outputs else jax.ShapeDtypeStruct((2, 1, size, size), jnp.float32),
            in_specs=([smem] if placed else []) + [vmem] * inputs,
            scratch_shapes=scratches,
        )

    count = lax.axis_size("space")
    position = lax.axis_index("space")
    half = count // 2
    is_left = position < half
    is_middle = (position == half - 1) | (position == half) if half else position == 0
    place = jnp.stack([position, is_left.astype(jnp.int32), is_middle.astype(jnp.int32)]).astype(jnp.int32)

    from_right = lax.ppermute(coupling, "space", [(k + 1, k) for k in range(count - 1)])
    matrix, green = call(begin_kernel, True, 3, 2, scratch)(place, onsite, hopping, coupling)
    from_right, _ = lax.optimization_barrier((from_right, green))
    inner, inner_adj, outer, outer_adj = call(links_kernel, True, 2, 4)(place, coupling, from_right)

    inward = [(k, k + 1) for k in range(half - 1)] + [(k, k - 1) for k in range(half + 1, count)]
    reduced = matrix
    for _ in range(max(half, count - half) - 1):
        incoming = lax.ppermute(green, "space", inward)
        reduced, green = call(advance_kernel, False, 4, 2, scratch)(matrix, incoming, inner, inner_adj)

    meeting = [(half - 1, half), (half, half - 1)] if half else []
    incoming = lax.ppermute(green, "space", meeting)
    full, before, after = call(meet_kernel, True, 5, 3, scratch)(place, reduced, green, incoming, outer, outer_adj)

    outward = [(k, k - 1) for k in range(1, half)] + [(k, k + 1) for k in range(half, count - 1)]
    result = full[:, None]
    for _ in range(max(half, count - half) - 1):
        incoming = lax.ppermute(result[:, 0], "space", outward)
        result = call(recede_kernel, True, 5, 0)(place, full, green, incoming, before, after)
    return result


def choose(condition, former, latter):
    return jnp.where(condition, former[0], latter[0]), jnp.where(condition, former[1], latter[1])


def whereabouts():
    position = lax.axis_index("space")
    return position < 2, (position == 0) | (position == 3)


def slab_kernel(onsite, hopping, coupling, slab):
    size = hopping.shape[-1]
    diagonal = lax.broadcasted_iota(jnp.int32, (size, size), 0) == lax.broadcasted_iota(jnp.int32, (size, size), 1)
    for part in range(2):
        slab[part] = jnp.where(diagonal, jnp.broadcast_to(onsite[part], (size, size)), 0.0) - hopping[part, 0]
        slab[2 + part] = coupling[part, 0]


def end_kernel(slab, own, link_adj, message, before, re, im):
    is_left, is_outer = whereabouts()
    link = slab.at[pl.ds(2, 2)]
    store(own, load(slab))
    store(link_adj, adjoint(load(link)))

    @pl.when(is_outer)
    def _():
        @pl.when(is_left)
        def _():
            pr, pi = complex_product(load(link_adj), load(link), dot_halves)
            own[0] = own[0] - pi
            own[1] = own[1] + pr

        green = inverse(load(own), re, im)
        store(own, green)
        store(message, green)

        @pl.when(jnp.logical_not(is_left))
        def _():
            store(before, complex_product(load(own), load(link_adj)))
            store(message, complex_product(load(link), load(before), dot_halves))


def send_half(is_left, middle, middle_adj, green, message):
    store(message, green)

    @pl.when(jnp.logical_not(is_left))
    def _():
        inside = complex_product(load(message), load(middle_adj), dot_halves)
        store(message, complex_product(load(middle), inside, dot_halves))


def outer_kernel(inner, own, sigma, before, reduced, theirs_adj, before_out, message, re, im):
    is_left, is_outer = whereabouts()

    @pl.when(is_outer)
    def _():
        theirs = inner.at[pl.ds(2, 2)]
        store(theirs_adj, adjoint(load(theirs)))
        store(reduced, load(sigma))
        store(before_out, load(before))

        @pl.when(is_left)
        def _():
            store(before_out, complex_product(load(own), load(theirs)))
            store(reduced, complex_product(load(theirs_adj), load(before_out), dot_halves))

        value = minus(load(inner), load(reduced))
        store(reduced, value)
        send_half(is_left, theirs, theirs_adj, inverse(value, re, im), message)


def inner_kernel(slab, link_adj, incoming, outer_reduced, outer_message, reduced, message, re, im):
    is_left, is_outer = whereabouts()
    link = slab.at[pl.ds(2, 2)]

    @pl.when(is_outer)
    def _():
        store(reduced, load(outer_reduced))
        store(message, load(outer_message))

    @pl.when(jnp.logical_not(is_outer))
    def _():
        store(reduced, load(incoming))

        @pl.when(is_left)
        def _():
            inside = complex_product(load(incoming), load(link), dot_halves)
            store(reduced, complex_product(load(link_adj), inside, dot_halves))

        value = minus(load(slab), load(reduced))
        store(reduced, value)
        send_half(is_left, link, link_adj, inverse(value, re, im), message)


def factor_kernel(own, slab, theirs_adj, after):
    is_left, is_outer = whereabouts()

    @pl.when(is_outer)
    def _():
        store(after, complex_product(choose(is_left, load(theirs_adj), load(slab.at[pl.ds(2, 2)])), load(own)))


def close_kernel(
    own, slab, link_adj, inner, theirs_adj, before, after, reduced, incoming, out, full, re, im
):
    is_left, is_outer = whereabouts()
    store(full, load(incoming))

    @pl.when(jnp.logical_not(is_left))
    def _():
        middle = choose(is_outer, load(inner.at[pl.ds(2, 2)]), load(slab.at[pl.ds(2, 2)]))
        middle_adj = choose(is_outer, load(theirs_adj), load(link_adj))
        inside = complex_product(load(incoming), middle, dot_halves)
        store(full, complex_product(middle_adj, inside, dot_halves))

    green = inverse(minus(load(reduced), load(full)), re, im, refine=True)

    @pl.when(jnp.logical_not(is_outer))
    def _():
        out[0, 0] = green[0]
        out[1, 0] = green[1]

    @pl.when(is_outer)
    def _():
        store(full, green)
        change = complex_product(complex_product(load(before), load(full)), load(after))
        out[0, 0] = own[0] + change[0]
        out[1, 0] = own[1] + change[1]


def four_slabs(onsite, hopping, coupling):
    size = onsite.shape[-1]
    scratch = [pltpu.VMEM((size, size), jnp.float32)] * 2
    within_halves = [(0, 1), (1, 0), (2, 3), (3, 2)]
    across = [(0, 3), (3, 0), (1, 2), (2, 1)]

    def on_chip(value):
        return pltpu.with_memory_space_constraint(value, pltpu.VMEM)

    def call(kernel, outputs, scratch_shapes, *operands):
        vmem = pl.BlockSpec(memory_space=pltpu.VMEM)
        results = pl.pallas_call(
            kernel,
            out_shape=[pltpu.VMEM((planes, size, size), jnp.float32) for planes in outputs],
            in_specs=[vmem] * len(operands),
            scratch_shapes=scratch_shapes,
        )(*operands)
        return [on_chip(value) for value in results]

    def move(value, pairs):
        return on_chip(lax.ppermute(value, "space", pairs))

    slab = call(slab_kernel, [4], [], onsite, hopping, coupling)[0]
    inner = move(slab, within_halves)
    own, link_adj, message, before = call(end_kernel, [2] * 4, scratch, slab)
    incoming = move(message, within_halves)
    reduced, theirs_adj, before, message = call(outer_kernel, [2] * 4, scratch, inner, own, message, before)
    reduced, message = call(inner_kernel, [2] * 2, scratch, slab, link_adj, incoming, reduced, message)
    incoming = move(message, across)
    late_own, _ = lax.optimization_barrier((own, message))
    after = call(factor_kernel, [2], [], on_chip(late_own), slab, theirs_adj)[0]
    vmem = pl.BlockSpec(memory_space=pltpu.VMEM)
    return pl.pallas_call(
        close_kernel,
        out_shape=jax.ShapeDtypeStruct(hopping.shape, jnp.float32),
        in_specs=[vmem] * 9,
        scratch_shapes=[pltpu.VMEM((2, size, size), jnp.float32)] + scratch,
    )(own, slab, link_adj, inner, theirs_adj, before, after, reduced, incoming)


def on_device(onsite, hopping, coupling):
    assert onsite.shape[1] == 1
    if lax.axis_size("space") == 4:
        return four_slabs(onsite, hopping, coupling)
    return chain_of_slabs(onsite, hopping, coupling)


def solution(mesh):
    return jax.shard_map(
        on_device,
        mesh=mesh,
        in_specs=(
            P("energy", "space", None),
            P("energy", "space", None, None),
            P("energy", "space", None, None),
        ),
        out_specs=P("energy", "space", None, None),
        check_vma=False,
    )
```

```python
import functools

import jax
import jax.numpy as jnp
from jax import lax
from jax.experimental import pallas as pl
from jax.experimental.pallas import tpu as pltpu
from jax.sharding import PartitionSpec as P

TILE = 8


def dot_full(former, latter):
    return jnp.dot(former, latter, precision=lax.Precision.HIGHEST, preferred_element_type=jnp.float32)


def halves(value):
    high = value.astype(jnp.bfloat16)
    return high, (value - high.astype(jnp.float32)).astype(jnp.bfloat16)


def dot_halves(former, latter):
    former_high, former_low = halves(former)
    latter_high, latter_low = halves(latter)
    dot = functools.partial(jnp.dot, preferred_element_type=jnp.float32)
    return dot(former_high, latter_high) + (dot(former_high, latter_low) + dot(former_low, latter_high))


def complex_product(former, latter, dot=dot_full):
    columns = latter[0].shape[1]
    wide = jnp.concatenate(former, axis=1)
    top = jnp.concatenate(latter, axis=1)
    bottom = jnp.concatenate([-latter[1], latter[0]], axis=1)
    both = dot(wide, jnp.concatenate([top, bottom], axis=0))
    return both[:, :columns], both[:, columns:]


def adjoint(value):
    return value[0].T, -value[1].T


def minus(former, latter):
    return former[0] - latter[0], former[1] - latter[1]


def plus(former, latter):
    return former[0] + latter[0], former[1] + latter[1]


def load(ref):
    return ref[0], ref[1]


def store(ref, value):
    ref[0] = value[0]
    ref[1] = value[1]


def times(ar, ai, br, bi):
    return ar * br - ai * bi, ar * bi + ai * br


def gauss_jordan(re, im):
    size = re.shape[0]
    lane = lax.broadcasted_iota(jnp.int32, (TILE, size), 1)
    sub = lax.broadcasted_iota(jnp.int32, (TILE, size), 0)
    lane_all = lax.broadcasted_iota(jnp.int32, (size, size), 1)

    def column(value, index):
        return jnp.broadcast_to(value[:, index : index + 1], (TILE, size))

    def row(value, index):
        return jnp.broadcast_to(value[index : index + 1, :], (TILE, size))

    past = None
    for start in range(0, size, TILE):
        stop = start + TILE
        pr, pi = re[start:stop, :], im[start:stop, :]
        if past is not None:
            first = start - TILE
            own = (lane >= first) & (lane < start)
            terms = [
                times(column(pr, first + k), column(pi, first + k), row(past[0], k), row(past[1], k))
                for k in range(TILE)
            ]
            while len(terms) > 1:
                terms = [plus(a, b) for a, b in zip(terms[::2], terms[1::2])]
            pr, pi = minus((jnp.where(own, 0.0, pr), jnp.where(own, 0.0, pi)), terms[0])
        spread = [
            (
                jnp.where(sub > TILE, 0.0, column(pr, start + j)),
                jnp.where(sub > TILE, 0.0, column(pi, start + j)),
            )
            for j in range(TILE)
        ]
        pivot_re = pivot_im = pivot_scale = None
        for j in range(TILE):
            br, bi = spread[j]
            xr, xi = row(br, j), row(bi, j)
            scale = 1.0 / (xr * xr + xi * xi)
            at_row = sub == j
            wr = jnp.where(at_row, 0.0, (br * xr + bi * xi) * scale)
            wi = jnp.where(at_row, 0.0, (bi * xr - br * xi) * scale)
            for k in range(j + 1, TILE):
                yr, yi = spread[k]
                spread[k] = minus((yr, yi), times(wr, wi, row(yr, j), row(yi, j)))
            at_lane = lane == start + j
            tr, ti = times(wr, wi, row(pr, j), row(pi, j))
            pr = jnp.where(at_lane, jnp.where(at_row, 1.0, -wr), pr - tr)
            pi = jnp.where(at_lane, -wi, pi - ti)
            if j:
                xr = jnp.where(at_row, xr, pivot_re)
                xi = jnp.where(at_row, xi, pivot_im)
                scale = jnp.where(at_row, scale, pivot_scale)
            pivot_re, pivot_im, pivot_scale = xr, xi, scale
        pr, pi = times(pr, pi, pivot_re * pivot_scale, -(pivot_im * pivot_scale))
        ar, ai = re[...], im[...]

        def padded(value, start=start, stop=stop):
            blocks = [value]
            if start:
                blocks.insert(0, jnp.zeros((start, size), jnp.float32))
            if stop < size:
                blocks.append(jnp.zeros((size - stop, size), jnp.float32))
            return jnp.concatenate(blocks, axis=0)

        ur, ui = complex_product((ar, ai), (padded(pr), padded(pi)), dot_halves)
        own = (lane_all >= start) & (lane_all < stop)
        nr = jnp.where(own, 0.0, ar) - ur
        ni = jnp.where(own, 0.0, ai) - ui
        for low, high in ((0, start), (min(stop + TILE, size), size)):
            if high > low:
                re[low:high, :] = nr[low:high]
                im[low:high, :] = ni[low:high]
        re[start:stop, :] = pr
        im[start:stop, :] = pi
        past = (pr, pi)


def refined(matrix, estimate):
    size = estimate[0].shape[0]
    diagonal = lax.broadcasted_iota(jnp.int32, (size, size), 0) == lax.broadcasted_iota(jnp.int32, (size, size), 1)
    pr, pi = complex_product(matrix, estimate)
    rest = jnp.where(diagonal, 1.0, 0.0) - pr, -pi
    return plus(estimate, complex_product(estimate, rest, dot_halves))


def inverse(matrix, re, im, refine=False):
    re[...] = matrix[0]
    im[...] = matrix[1]
    gauss_jordan(re, im)
    result = re[...], im[...]
    return refined(matrix, result) if refine else result


def begin_kernel(place, onsite, hopping, coupling, matrix, green, re, im):
    size = re.shape[0]
    diagonal = lax.broadcasted_iota(jnp.int32, (size, size), 0) == lax.broadcasted_iota(jnp.int32, (size, size), 1)
    for part in range(2):
        spread = jnp.broadcast_to(onsite[part], (size, size))
        matrix[part] = jnp.where(diagonal, spread, 0.0) - hopping[part, 0]

    @pl.when(place[0] == 0)
    def _():
        link = coupling[0, 0], coupling[1, 0]
        pr, pi = complex_product(adjoint(link), link)
        matrix[0] = matrix[0] - pi
        matrix[1] = matrix[1] + pr

    store(green, inverse(load(matrix), re, im, refine=True))


def links_kernel(place, coupling, behind, inner, inner_adj, outer, outer_adj):
    own = coupling[0, 0], coupling[1, 0]
    other = behind[0, 0], behind[1, 0]

    @pl.when(place[1] == 1)
    def _():
        store(inner, own)
        store(inner_adj, adjoint(own))
        store(outer, adjoint(other))
        store(outer_adj, other)

    @pl.when(place[1] == 0)
    def _():
        store(outer, own)
        store(outer_adj, adjoint(own))
        store(inner, adjoint(other))
        store(inner_adj, other)


def advance_kernel(matrix, incoming, link, link_adj, reduced, green, re, im):
    sigma = complex_product(load(link_adj), complex_product(load(incoming), load(link)))
    value = minus(load(matrix), sigma)
    store(reduced, value)
    store(green, inverse(value, re, im, refine=True))


def meet_kernel(place, reduced, green, incoming, link, link_adj, full, before, after, re, im):
    @pl.when(place[2] == 1)
    def _():
        sigma = complex_product(load(link_adj), complex_product(load(incoming), load(link)))
        store(full, inverse(minus(load(reduced), sigma), re, im, refine=True))

    @pl.when(place[2] == 0)
    def _():
        store(full, load(green))
        store(before, complex_product(load(green), load(link_adj)))
        store(after, complex_product(load(link), load(green)))


def recede_kernel(place, full, green, incoming, before, after, out):
    @pl.when(place[2] == 1)
    def _():
        for part in range(2):
            out[part, 0] = full[part]

    @pl.when(place[2] == 0)
    def _():
        change = complex_product(complex_product(load(before), load(incoming)), load(after))
        value = plus(load(green), change)
        for part in range(2):
            out[part, 0] = value[part]


def chain_of_slabs(onsite, hopping, coupling):
    size = onsite.shape[-1]
    pair = jax.ShapeDtypeStruct((2, size, size), jnp.float32)
    scratch = [pltpu.VMEM((size, size), jnp.float32)] * 2
    smem = pl.BlockSpec(memory_space=pltpu.SMEM)
    vmem = pl.BlockSpec(memory_space=pltpu.VMEM)

    def call(kernel, placed, inputs, outputs, scratches=(), **options):
        return pl.pallas_call(
            kernel,
            out_shape=(pair,) * outputs if outputs else jax.ShapeDtypeStruct((2, 1, size, size), jnp.float32),
            in_specs=([smem] if placed else []) + [vmem] * inputs,
            scratch_shapes=scratches,
        )

    count = lax.axis_size("space")
    position = lax.axis_index("space")
    half = count // 2
    is_left = position < half
    is_middle = (position == half - 1) | (position == half) if half else position == 0
    place = jnp.stack([position, is_left.astype(jnp.int32), is_middle.astype(jnp.int32)]).astype(jnp.int32)

    from_right = lax.ppermute(coupling, "space", [(k + 1, k) for k in range(count - 1)])
    matrix, green = call(begin_kernel, True, 3, 2, scratch)(place, onsite, hopping, coupling)
    from_right, _ = lax.optimization_barrier((from_right, green))
    inner, inner_adj, outer, outer_adj = call(links_kernel, True, 2, 4)(place, coupling, from_right)

    inward = [(k, k + 1) for k in range(half - 1)] + [(k, k - 1) for k in range(half + 1, count)]
    reduced = matrix
    for _ in range(max(half, count - half) - 1):
        incoming = lax.ppermute(green, "space", inward)
        reduced, green = call(advance_kernel, False, 4, 2, scratch)(matrix, incoming, inner, inner_adj)

    meeting = [(half - 1, half), (half, half - 1)] if half else []
    incoming = lax.ppermute(green, "space", meeting)
    full, before, after = call(meet_kernel, True, 5, 3, scratch)(place, reduced, green, incoming, outer, outer_adj)

    outward = [(k, k - 1) for k in range(1, half)] + [(k, k + 1) for k in range(half, count - 1)]
    result = full[:, None]
    for _ in range(max(half, count - half) - 1):
        incoming = lax.ppermute(result[:, 0], "space", outward)
        result = call(recede_kernel, True, 5, 0)(place, full, green, incoming, before, after)
    return result


def choose(condition, former, latter):
    return jnp.where(condition, former[0], latter[0]), jnp.where(condition, former[1], latter[1])


def whereabouts():
    position = lax.axis_index("space")
    return position < 2, (position == 0) | (position == 3)


def slab_kernel(onsite, hopping, coupling, slab, parcel):
    size = hopping.shape[-1]
    row = lax.broadcasted_iota(jnp.int32, (size, size), 0)
    lane = lax.broadcasted_iota(jnp.int32, (size, size), 1)
    for part in range(2):
        spread = jnp.broadcast_to(onsite[part], (size, size))
        slab[part] = jnp.where(row == lane, spread, 0.0) - hopping[part, 0]
        slab[2 + part] = coupling[part, 0]
        parcel[pl.ds(size + TILE + part * size, size), :] = coupling[part, 0]
    parcel[pl.ds(0, size), :] = jnp.where(row > lane, slab[1], slab[0])
    parcel[pl.ds(size, TILE), :] = jnp.broadcast_to(onsite[1], (TILE, size))


def unpack(parcel, slab):
    size = parcel.shape[-1]
    row = lax.broadcasted_iota(jnp.int32, (size, size), 0)
    lane = lax.broadcasted_iota(jnp.int32, (size, size), 1)
    both = parcel[pl.ds(0, size), :]
    turned = both.T
    diagonal = jnp.broadcast_to(parcel[pl.ds(size, 1), :], (size, size))
    slab[0] = jnp.where(row > lane, turned, both)
    slab[1] = jnp.where(row > lane, both, jnp.where(row < lane, -turned, diagonal))
    for part in range(2):
        slab[2 + part] = parcel[pl.ds(size + TILE + part * size, size), :]


def end_kernel(slab, own, link_adj, message, re, im):
    is_left, is_outer = whereabouts()
    link = slab.at[pl.ds(2, 2)]
    store(own, load(slab))
    store(link_adj, adjoint(load(link)))

    @pl.when(is_outer)
    def _():
        @pl.when(is_left)
        def _():
            pr, pi = complex_product(load(link_adj), load(link), dot_halves)
            own[0] = own[0] - pi
            own[1] = own[1] + pr

        green = inverse(load(own), re, im)
        store(own, green)
        store(message, green)

        @pl.when(jnp.logical_not(is_left))
        def _():
            inside = complex_product(load(own), load(link_adj), dot_halves)
            store(message, complex_product(load(link), inside, dot_halves))


def send_half(is_left, middle, middle_adj, green, message):
    store(message, green)

    @pl.when(jnp.logical_not(is_left))
    def _():
        inside = complex_product(load(message), load(middle_adj), dot_halves)
        store(message, complex_product(load(middle), inside, dot_halves))


def outer_kernel(parcel, own, sigma, inner, reduced, theirs_adj, message, re, im):
    is_left, is_outer = whereabouts()

    @pl.when(is_outer)
    def _():
        unpack(parcel, inner)
        theirs = inner.at[pl.ds(2, 2)]
        store(theirs_adj, adjoint(load(theirs)))
        store(reduced, load(sigma))

        @pl.when(is_left)
        def _():
            inside = complex_product(load(own), load(theirs), dot_halves)
            store(reduced, complex_product(load(theirs_adj), inside, dot_halves))

        value = minus(load(inner), load(reduced))
        store(reduced, value)
        send_half(is_left, theirs, theirs_adj, inverse(value, re, im), message)


def inner_kernel(slab, link_adj, incoming, outer_reduced, outer_message, reduced, message, re, im):
    is_left, is_outer = whereabouts()
    link = slab.at[pl.ds(2, 2)]

    @pl.when(is_outer)
    def _():
        store(reduced, load(outer_reduced))
        store(message, load(outer_message))

    @pl.when(jnp.logical_not(is_outer))
    def _():
        store(reduced, load(incoming))

        @pl.when(is_left)
        def _():
            inside = complex_product(load(incoming), load(link), dot_halves)
            store(reduced, complex_product(load(link_adj), inside, dot_halves))

        value = minus(load(slab), load(reduced))
        store(reduced, value)
        send_half(is_left, link, link_adj, inverse(value, re, im), message)


def factor_kernel(own, slab, link_adj, inner, theirs_adj, before, after):
    is_left, is_outer = whereabouts()

    @pl.when(is_outer)
    def _():
        link, theirs = load(slab.at[pl.ds(2, 2)]), load(inner.at[pl.ds(2, 2)])
        store(before, complex_product(load(own), choose(is_left, theirs, load(link_adj))))
        store(after, complex_product(choose(is_left, load(theirs_adj), link), load(own)))


def close_kernel(
    own, slab, link_adj, inner, theirs_adj, before, after, reduced, incoming, out, full, re, im
):
    is_left, is_outer = whereabouts()
    store(full, load(incoming))

    @pl.when(jnp.logical_not(is_left))
    def _():
        middle = choose(is_outer, load(inner.at[pl.ds(2, 2)]), load(slab.at[pl.ds(2, 2)]))
        middle_adj = choose(is_outer, load(theirs_adj), load(link_adj))
        inside = complex_product(load(incoming), middle, dot_halves)
        store(full, complex_product(middle_adj, inside, dot_halves))

    green = inverse(minus(load(reduced), load(full)), re, im)

    @pl.when(jnp.logical_not(is_outer))
    def _():
        out[0, 0] = green[0]
        out[1, 0] = green[1]

    @pl.when(is_outer)
    def _():
        value = minus(load(reduced), load(full))
        store(full, refined(value, (re[...], im[...])))
        change = complex_product(complex_product(load(before), load(full)), load(after))
        out[0, 0] = own[0] + change[0]
        out[1, 0] = own[1] + change[1]


def four_slabs(onsite, hopping, coupling):
    size = onsite.shape[-1]
    scratch = [pltpu.VMEM((size, size), jnp.float32)] * 2
    within_halves = [(0, 1), (1, 0), (2, 3), (3, 2)]
    across = [(0, 3), (3, 0), (1, 2), (2, 1)]

    def on_chip(value):
        return pltpu.with_memory_space_constraint(value, pltpu.VMEM)

    def call(kernel, outputs, scratch_shapes, *operands):
        vmem = pl.BlockSpec(memory_space=pltpu.VMEM)
        results = pl.pallas_call(
            kernel,
            out_shape=[pltpu.VMEM(shape, jnp.float32) for shape in outputs],
            in_specs=[vmem] * len(operands),
            scratch_shapes=scratch_shapes,
        )(*operands)
        return [on_chip(value) for value in results]

    def move(value, pairs):
        return on_chip(lax.ppermute(value, "space", pairs))

    pair, double = (2, size, size), (4, size, size)
    parcel_shape = (3 * size + TILE, size)
    slab, parcel = call(slab_kernel, [double, parcel_shape], [], onsite, hopping, coupling)
    parcel = move(parcel, within_halves)
    own, link_adj, message = call(end_kernel, [pair] * 3, scratch, slab)
    incoming = move(message, within_halves)
    inner, reduced, theirs_adj, message = call(outer_kernel, [double] + [pair] * 3, scratch, parcel, own, message)
    reduced, message = call(inner_kernel, [pair] * 2, scratch, slab, link_adj, incoming, reduced, message)
    incoming = move(message, across)
    late_own, _ = lax.optimization_barrier((own, message))
    before, after = call(
        factor_kernel, [pair] * 2, [], on_chip(late_own), slab, link_adj, inner, theirs_adj
    )
    vmem = pl.BlockSpec(memory_space=pltpu.VMEM)
    return pl.pallas_call(
        close_kernel,
        out_shape=jax.ShapeDtypeStruct(hopping.shape, jnp.float32),
        in_specs=[vmem] * 9,
        scratch_shapes=[pltpu.VMEM((2, size, size), jnp.float32)] + scratch,
    )(own, slab, link_adj, inner, theirs_adj, before, after, reduced, incoming)


def on_device(onsite, hopping, coupling):
    assert onsite.shape[1] == 1
    if lax.axis_size("space") == 4:
        return four_slabs(onsite, hopping, coupling)
    return chain_of_slabs(onsite, hopping, coupling)


def solution(mesh):
    return jax.shard_map(
        on_device,
        mesh=mesh,
        in_specs=(
            P("energy", "space", None),
            P("energy", "space", None, None),
            P("energy", "space", None, None),
        ),
        out_specs=P("energy", "space", None, None),
        check_vma=False,
    )
```
